32 devices in a mesh: row: 8 (over z, y), col: 4 (over x, core).
Axes of the slice: x: 2, y: 2, z: 4, core: 2. Of those that a mesh axis runs over, the one named last changes fastest.
Arguments:
- inv_blocks: bfloat16 [2048, 2048], P('row', 'col'), may hold values from -0.125 to 0.125
- factor: bfloat16 [4, 2048, 128], P('col', 'row'), may hold values from -2.3125 to 2.3125
- pattern: int32 [4, 16], P('col', 'row'), may hold values from 0 to 1, as said below
- diag_inv: float32 [4, 128, 128], P(None, 'row', 'col'), may hold values from -12 to 12
Outputs:
- inverse_panel: bfloat16 [4, 128, 2048], P(None, 'col', 'row')
- diag_block: float32 [4, 128, 128], P(None, 'row', 'col')
The draws below stay inside these ranges and needn't reach their ends.
Inputs may be any that keep to these rules, and one draw needn't show every extreme that they name: pattern is 0 or 1; each supernode has its own share of 1s.
All inputs are finite; a program needn't handle non-finite values.
Results may differ from the reference program's by a relative error of at most 0.0005.
Values may be sent and summed in bfloat16 or wider, within the bound.
No kernel may reach another device: no remote copies, remote signals or barrier semaphores. Data moves between devices by JAX's collectives and lax.ppermute only.
A program may use at most 64 MiB of HBM per device.

```python
import jax
import jax.numpy as jnp
from jax import lax

W = 128
NB = 16
M = 2048
S = 4
N_COL = 4


def draw_pattern(key, part):
    first = jax.random.fold_in(key, 11)
    second = jax.random.fold_in(key, 23)
    level = jax.random.randint(first, (S, 1), 2, 10)
    votes = jax.random.randint(second, (S, NB), 0, 10)
    return (votes < level).astype(jnp.int32)


def block_scale(rng, dims, pieces, smallest, top_value):
    factor_of, own = 1.0, jax.random.fold_in(rng, 6)
    for position, shards_of in pieces:
        draws = jnp.exp(jax.random.uniform(jax.random.fold_in(own, position), (shards_of,), jnp.float32, smallest / len(pieces), top_value / len(pieces)))
        factor_of = factor_of * jnp.repeat(draws, dims[position] // shards_of).reshape([-1 if axis == position else 1 for axis in range(len(dims))])
    return factor_of


def scatter_about(rng, dims, deviation, limit, cuts=(), kind=jnp.bfloat16):
    factor_of = block_scale(rng, dims, cuts, -0.22, 0.18) if cuts else 1.0
    array = jax.random.normal(rng, dims, jnp.float32) * deviation * factor_of
    return jnp.minimum(jnp.maximum(array, -limit), limit).astype(kind)


def setup_inputs(seed: int = 0) -> dict:
    key_list = jax.random.split(jax.random.key(seed), 5)
    return {
        "inv_blocks": scatter_about(key_list[0], (M, M), M ** -0.5, 0.125, ((0, 8), (1, 4))),
        "factor": scatter_about(key_list[1], (S, M, W), (M ** -0.125), 2.3125, ((0, 4), (1, 8))),
        "pattern": draw_pattern(jax.random.fold_in(key_list[4], 71), 0),
        "diag_inv": scatter_about(key_list[3], (S, W, W), 2.0, 12.0, ((1, 8), (2, 4)), jnp.float32),
    }


def reference(inv_blocks, factor, pattern, diag_inv):
    keep = jnp.repeat(pattern, W, axis=1).astype(jnp.bfloat16)
    masked = factor * keep[:, :, None]
    span = M // N_COL

    def add_range(index, total):
        start = index * span
        block_a = lax.dynamic_slice_in_dim(inv_blocks, start, span, 1).astype(jnp.float32)
        block_l = lax.dynamic_slice_in_dim(masked, start, span, 1).astype(jnp.float32)
        product = jnp.einsum('ij,sjw->siw', block_a, block_l)
        return total - product

    panel_sum = lax.fori_loop(0, N_COL, add_range, jnp.zeros((S, M, W), jnp.float32))
    inverse_panel = jnp.transpose(panel_sum, (0, 2, 1)).astype(jnp.bfloat16)
    inner = jnp.einsum('siw,siv->swv', masked.astype(jnp.float32), panel_sum, precision=lax.Precision.HIGHEST)
    return inverse_panel, diag_inv - inner
```

```python
import functools

import jax
import jax.numpy as jnp
from jax import lax
from jax.experimental import pallas as pl
from jax.experimental.pallas import tpu as pltpu
from jax.sharding import PartitionSpec as P


def swap(block, axis, distance):
    size = lax.axis_size(axis)
    return lax.ppermute(block, axis, [(i, i ^ distance) for i in range(size)])


def product_kernel(n_col, *refs):
    blocks = refs[:n_col]
    rows_ref, own_ref, panel_ref, inner_ref = refs[n_col:]
    col = lax.axis_index("col")
    span = blocks[0].shape[1]
    total = jnp.zeros(own_ref.shape, jnp.float32)
    for distance in range(n_col):
        start = pl.multiple_of((col ^ distance) * span, span)
        total += jnp.dot(
            blocks[distance][...],
            rows_ref[pl.ds(start, span), :],
            preferred_element_type=jnp.float32,
        )
    panel = -total
    panel_ref[...] = jnp.transpose(panel).astype(jnp.bfloat16)
    high = panel.astype(jnp.bfloat16)
    low = (panel - high.astype(jnp.float32)).astype(jnp.bfloat16)
    own = own_ref[...]
    dims = (((0,), (0,)), ((), ()))
    inner_ref[...] = lax.dot_general(
        own, high, dims, preferred_element_type=jnp.float32
    ) + lax.dot_general(own, low, dims, preferred_element_type=jnp.float32)


def on_device(inv_blocks, factor, pattern, diag_inv):
    n_row = lax.axis_size("row")
    n_col = lax.axis_size("col")
    rows, width = factor.shape[1:]
    row = lax.axis_index("row")
    col = lax.axis_index("col")

    keep = jnp.repeat(pattern, width, axis=1).astype(jnp.bfloat16)
    own = (factor * keep[:, :, None])[0]

    blocks = [None] * n_col
    blocks[0] = inv_blocks
    for distance in range(2, n_col, 2):
        blocks[distance] = swap(inv_blocks, "col", distance)
    for distance in range(0, n_col, 2):
        blocks[distance + 1] = swap(blocks[distance], "col", 1)

    held = [None] * n_row
    held[0] = own
    for distance in range(2, n_row, 2):
        held[distance] = swap(own, "row", distance)
    for distance in range(0, n_row, 2):
        held[distance + 1] = swap(held[distance], "row", 1)
    level = jnp.zeros((n_row, rows, width), jnp.bfloat16)
    for distance in range(n_row):
        level = lax.dynamic_update_index_in_dim(level, held[distance], row ^ distance, 0)

    vmem = pl.BlockSpec(memory_space=pltpu.VMEM)
    panel, inner = pl.pallas_call(
        functools.partial(product_kernel, n_col),
        out_shape=(
            jax.ShapeDtypeStruct((width, rows), jnp.bfloat16),
            jax.ShapeDtypeStruct((width, width), jnp.float32),
        ),
        in_specs=[vmem] * (n_col + 2),
        out_specs=(vmem, vmem),
        name="product",
    )(*blocks, level.reshape(n_row * rows, width), own)

    part = panel.reshape(n_col, width // n_col, rows)
    out = jnp.zeros((n_col, width // n_col, rows), jnp.bfloat16)
    for distance in range(n_col):
        piece = lax.dynamic_index_in_dim(part, col ^ distance, 0, keepdims=False)
        if distance:
            piece = swap(piece, "col", distance)
        out = lax.dynamic_update_index_in_dim(out, piece, col ^ distance, 0)

    tall, wide = width // n_row, width // n_col
    packed = inner.reshape(n_row, tall, n_col, wide).transpose(0, 2, 1, 3)
    packed = packed.reshape(n_row * n_col, tall * wide // 128, 128) if tall * wide % 128 == 0 else packed.reshape(n_row * n_col, 1, tall * wide)
    packed = lax.all_to_all(packed, ("row", "col"), 0, 0, tiled=True)
    inner_sum = packed.reshape(n_row, n_col, tall, wide).sum(0)
    return out, diag_inv - inner_sum


def solution(mesh):
    return jax.shard_map(
        on_device,
        mesh=mesh,
        in_specs=(P("row", "col"), P("col", "row", None), P("col", "row"), P(None, "row", "col")),
        out_specs=(P(None, "col", "row"), P(None, "row", "col")),
        check_vma=False,
    )
```

```python
import functools

import jax
import jax.numpy as jnp
from jax import lax
from jax.experimental import pallas as pl
from jax.experimental.pallas import tpu as pltpu
from jax.sharding import PartitionSpec as P

VMEM = pl.BlockSpec(memory_space=pltpu.VMEM)
PARAMS = pltpu.CompilerParams(vmem_limit_bytes=16 * 2**20)
LANES = 128


def in_hbm(array):
    return pltpu.with_memory_space_constraint(array, pltpu.HBM)


def swap(block, axis, distance):
    size = lax.axis_size(axis)
    return lax.ppermute(block, axis, [(i, i ^ distance) for i in range(size)])


def mask_kernel(pattern_ref, factor_ref, own_ref, keep_ref, rows_ref, sem):
    width = factor_ref.shape[2]
    copies = (
        pltpu.make_async_copy(factor_ref, rows_ref, sem.at[0]),
        pltpu.make_async_copy(pattern_ref, keep_ref, sem.at[1]),
    )
    for copy in copies:
        copy.start()
    for copy in copies:
        copy.wait()
    for block in range(keep_ref.shape[1]):
        rows = pl.ds(block * width, width)
        keep = keep_ref[0, block].astype(jnp.float32).astype(jnp.bfloat16)
        own_ref[rows, :] = rows_ref[0, rows, :] * keep


def add_products(total, blocks, level_ref, half):
    n_col = len(blocks)
    col = lax.axis_index("col")
    rows = level_ref.shape[1]
    pairs = blocks[0].shape[1] // (2 * rows)
    for distance in range(n_col):
        for pair in range(pairs):
            start = pl.multiple_of((2 * pair + half) * rows, rows)
            part = jnp.dot(
                blocks[distance][:, pl.ds(start, rows)],
                level_ref[(col ^ distance) * pairs + pair],
                preferred_element_type=jnp.float32,
            )
            total = part if total is None else total + part
    return total


def near_kernel(n_col, *refs):
    blocks, (level_ref, total_ref) = refs[:n_col], refs[n_col:]
    total_ref[...] = add_products(None, blocks, level_ref, lax.axis_index("row") % 2)


def far_kernel(n_col, dense, *refs):
    blocks = refs[:n_col]
    level_ref, near_ref, own_ref = refs[n_col : n_col + 3]
    panel_ref, packed_ref = refs[n_col + 3 : n_col + 5]
    sends = refs[n_col + 5 : 2 * n_col + 4]
    turned_ref, inner_ref = refs[2 * n_col + 4 :]
    col = lax.axis_index("col")
    total = add_products(near_ref[...], blocks, level_ref, 1 - lax.axis_index("row") % 2)

    tall = turned_ref.shape[0] // n_col
    turned_ref[...] = jnp.transpose(-total).astype(jnp.bfloat16)
    panel_ref[col] = turned_ref[pl.ds(pl.multiple_of(col * tall, tall), tall), :]
    for distance in range(1, n_col):
        start = pl.multiple_of((col ^ distance) * tall, tall)
        sends[distance - 1][...] = turned_ref[pl.ds(start, tall), :]

    high = total.astype(jnp.bfloat16)
    low = (total - high.astype(jnp.float32)).astype(jnp.bfloat16)
    own = own_ref[...]
    dims = (((0,), (0,)), ((), ()))
    inner = lax.dot_general(own, high, dims, preferred_element_type=jnp.float32)
    inner += lax.dot_general(own, low, dims, preferred_element_type=jnp.float32)
    if not dense:
        packed_ref[...] = inner
        return
    inner_ref[...] = inner
    lane = lax.broadcasted_iota(jnp.int32, (8, LANES), 1) // 32
    for a in range(4):
        parts = [inner_ref[pl.ds(4 * a + b, 8, stride=16), :] for b in range(4)]
        for owner in range(4):
            piece = parts[owner]
            for b in range(4):
                if b != owner:
                    turned = pltpu.roll(parts[b], (b - owner) % 4 * 32, 1)
                    piece = jnp.where(lane == b, turned, piece)
            packed_ref[pl.ds(4 * owner + a, 8, stride=16), :] = piece


def close_kernel(packed_ref, diag_ref, out_ref):
    total = packed_ref[pl.ds(0, 16), :]
    for row in range(1, 8):
        total += packed_ref[pl.ds(16 * row, 16), :]
    for b in range(4):
        part = pltpu.roll(total, (4 - b) % 4 * 32, 1) if b else total
        rows = pl.ds(b, 16, stride=4)
        out_ref[rows, :] = diag_ref[rows, :] + part[:, :32]


def on_device(inv_blocks, factor, pattern, diag_inv):
    n_row = lax.axis_size("row")
    n_col = lax.axis_size("col")
    rows, width = factor.shape[1:]
    tall, wide = width // n_row, width // n_col
    dense = (width, n_row, n_col) == (LANES, 8, 4)
    high = lax.axis_index("row") // 2
    shape = jax.ShapeDtypeStruct

    own = pl.pallas_call(
        mask_kernel,
        out_shape=shape((rows, width), jnp.bfloat16),
        in_specs=[pl.BlockSpec(memory_space=pltpu.HBM)] * 2,
        out_specs=VMEM,
        scratch_shapes=[
            pltpu.SMEM(pattern.shape, pattern.dtype),
            pltpu.VMEM(factor.shape, factor.dtype),
            pltpu.SemaphoreType.DMA((2,)),
        ],
        compiler_params=PARAMS,
        name="mask",
    )(in_hbm(pattern), in_hbm(factor))

    blocks = [None] * n_col
    blocks[0] = inv_blocks
    for distance in range(2, n_col, 2):
        blocks[distance] = swap(inv_blocks, "col", distance)
    for distance in range(0, n_col, 2):
        blocks[distance + 1] = swap(blocks[distance], "col", 1)

    near = jnp.zeros((n_row // 2, rows, width), jnp.bfloat16)
    far = jnp.zeros((n_row // 2, rows, width), jnp.bfloat16)
    for distance in range(0, n_row, 2):
        held = swap(own, "row", distance) if distance else own
        place = high ^ (distance // 2)
        near = lax.dynamic_update_index_in_dim(near, held, place, 0)
        far = lax.dynamic_update_index_in_dim(far, swap(held, "row", 1), place, 0)

    total = pl.pallas_call(
        functools.partial(near_kernel, n_col),
        out_shape=shape((rows, width), jnp.float32),
        in_specs=[VMEM] * (n_col + 1),
        out_specs=VMEM,
        compiler_params=PARAMS,
        name="near",
    )(*blocks, near)
    panel, packed, *sends = pl.pallas_call(
        functools.partial(far_kernel, n_col, dense),
        out_shape=[
            shape((n_col, wide, rows), jnp.bfloat16),
            shape((width, width), jnp.float32),
        ] + [shape((wide, rows), jnp.bfloat16)] * (n_col - 1),
        in_specs=[VMEM] * (n_col + 3),
        out_specs=[VMEM] * (n_col + 1),
        scratch_shapes=[
            pltpu.VMEM((width, rows), jnp.bfloat16),
            pltpu.VMEM((width, width), jnp.float32),
        ],
        compiler_params=PARAMS,
        name="far",
    )(*blocks, far, total, own)

    col = lax.axis_index("col")
    for distance in range(1, n_col):
        piece = swap(sends[distance - 1], "col", distance)
        panel = lax.dynamic_update_index_in_dim(panel, piece, col ^ distance, 0)

    axes = ("row", "col")
    if dense:
        packed = packed.reshape(n_row * n_col, 4, LANES)
        packed = lax.all_to_all(packed, axes, 0, 0, tiled=True)
        diag_block = pl.pallas_call(
            close_kernel,
            out_shape=shape((n_col * tall, wide), jnp.float32),
            in_specs=[VMEM, VMEM],
            out_specs=VMEM,
            compiler_params=PARAMS,
            name="close",
        )(packed.reshape(width, width), diag_inv.reshape(n_col * tall, wide))
        return panel, diag_block.reshape(n_col, tall, wide)
    packed = packed.reshape(n_row, tall, n_col, wide).transpose(0, 2, 1, 3)
    packed = packed.reshape(n_row * n_col, 1, tall * wide)
    packed = lax.all_to_all(packed, axes, 0, 0, tiled=True)
    return panel, diag_inv + packed.reshape(n_row, n_col, tall, wide).sum(0)


def solution(mesh):
    return jax.shard_map(
        on_device,
        mesh=mesh,
        in_specs=(P("row", "col"), P("col", "row", None), P("col", "row"), P(None, "row", "col")),
        out_specs=(P(None, "col", "row"), P(None, "row", "col")),
        check_vma=False,
    )
```

```python
import functools

import jax
import jax.numpy as jnp
from jax import lax
from jax.experimental import pallas as pl
from jax.experimental.pallas import tpu as pltpu
from jax.sharding import PartitionSpec as P


VMEM = pl.BlockSpec(memory_space=pltpu.VMEM)
PARAMS = pltpu.CompilerParams(vmem_limit_bytes=16 * 2**20)
LANES = 128


def in_hbm(array):
    return pltpu.with_memory_space_constraint(array, pltpu.HBM)


def swap(block, axis, distance):
    size = lax.axis_size(axis)
    return lax.ppermute(block, axis, [(i, i ^ distance) for i in range(size)])


def mask_kernel(pattern_ref, factor_ref, own_ref, keep_ref, rows_ref, sem):
    width = factor_ref.shape[2]
    copies = (
        pltpu.make_async_copy(factor_ref, rows_ref, sem.at[0]),
        pltpu.make_async_copy(pattern_ref, keep_ref, sem.at[1]),
    )
    for copy in copies:
        copy.start()
    for copy in copies:
        copy.wait()
    for block in range(keep_ref.shape[1]):
        rows = pl.ds(block * width, width)
        keep = keep_ref[0, block].astype(jnp.float32).astype(jnp.bfloat16)
        own_ref[rows, :] = rows_ref[0, rows, :] * keep


def add_products(total, blocks, level_ref, half):
    n_col = len(blocks)
    col = lax.axis_index("col")
    rows = level_ref.shape[1]
    pairs = blocks[0].shape[1] // (2 * rows)
    for distance in range(n_col):
        for pair in range(pairs):
            start = pl.multiple_of((2 * pair + half) * rows, rows)
            part = jnp.dot(
                blocks[distance][:, pl.ds(start, rows)],
                level_ref[(col ^ distance) * pairs + pair],
                preferred_element_type=jnp.float32,
            )
            total = part if total is None else total + part
    return total


def near_kernel(n_col, *refs):
    blocks, (level_ref, total_ref) = refs[:n_col], refs[n_col:]
    total_ref[...] = add_products(None, blocks, level_ref, lax.axis_index("row") % 2)


def far_kernel(n_col, dense, *refs):
    blocks = refs[:n_col]
    level_ref, near_ref, own_ref = refs[n_col : n_col + 3]
    packed_ref = refs[n_col + 3]
    sends = refs[n_col + 4 : 2 * n_col + 4]
    turned_ref, inner_ref = refs[2 * n_col + 4 :]
    col = lax.axis_index("col")
    total = add_products(near_ref[...], blocks, level_ref, 1 - lax.axis_index("row") % 2)

    tall = turned_ref.shape[0] // n_col
    turned_ref[...] = jnp.transpose(-total).astype(jnp.bfloat16)
    for distance in range(n_col):
        start = pl.multiple_of((col ^ distance) * tall, tall)
        sends[distance][...] = turned_ref[pl.ds(start, tall), :]

    high = total.astype(jnp.bfloat16)
    low = (total - high.astype(jnp.float32)).astype(jnp.bfloat16)
    own = own_ref[...]
    dims = (((0,), (0,)), ((), ()))
    inner = lax.dot_general(own, high, dims, preferred_element_type=jnp.float32)
    inner += lax.dot_general(own, low, dims, preferred_element_type=jnp.float32)
    if not dense:
        packed_ref[...] = inner
        return
    inner_ref[...] = inner
    lane = lax.broadcasted_iota(jnp.int32, (8, LANES), 1) // 32
    for a in range(4):
        parts = [inner_ref[pl.ds(4 * a + b, 8, stride=16), :] for b in range(4)]
        for owner in range(4):
            piece = parts[owner]
            for b in range(4):
                if b != owner:
                    turned = pltpu.roll(parts[b], (b - owner) % 4 * 32, 1)
                    piece = jnp.where(lane == b, turned, piece)
            packed_ref[pl.ds(4 * owner + a, 8, stride=16), :] = piece


def close_kernel(packed_ref, diag_ref, out_ref):
    total = packed_ref[pl.ds(0, 16), :]
    for row in range(1, 8):
        total += packed_ref[pl.ds(16 * row, 16), :]
    for b in range(4):
        part = pltpu.roll(total, (4 - b) % 4 * 32, 1) if b else total
        rows = pl.ds(b, 16, stride=4)
        out_ref[rows, :] = diag_ref[rows, :] + part[:, :32]


def on_device(inv_blocks, factor, pattern, diag_inv):
    n_row = lax.axis_size("row")
    n_col = lax.axis_size("col")
    rows, width = factor.shape[1:]
    tall, wide = width // n_row, width // n_col
    dense = (width, n_row, n_col) == (LANES, 8, 4)
    high = lax.axis_index("row") // 2
    shape = jax.ShapeDtypeStruct

    own = pl.pallas_call(
        mask_kernel,
        out_shape=shape((rows, width), jnp.bfloat16),
        in_specs=[pl.BlockSpec(memory_space=pltpu.HBM)] * 2,
        out_specs=VMEM,
        scratch_shapes=[
            pltpu.SMEM(pattern.shape, pattern.dtype),
            pltpu.VMEM(factor.shape, factor.dtype),
            pltpu.SemaphoreType.DMA((2,)),
        ],
        compiler_params=PARAMS,
        name="mask",
    )(in_hbm(pattern), in_hbm(factor))

    blocks = [None] * n_col
    blocks[0] = inv_blocks
    for distance in range(2, n_col, 2):
        blocks[distance] = swap(inv_blocks, "col", distance)
    for distance in range(0, n_col, 2):
        blocks[distance + 1] = swap(blocks[distance], "col", 1)

    near = jnp.zeros((n_row // 2, rows, width), jnp.bfloat16)
    far = jnp.zeros((n_row // 2, rows, width), jnp.bfloat16)
    for distance in range(0, n_row, 2):
        held = swap(own, "row", distance) if distance else own
        place = high ^ (distance // 2)
        near = lax.dynamic_update_index_in_dim(near, held, place, 0)
        held = swap(held, "row", 1)
        far = lax.dynamic_update_index_in_dim(far, held, place, 0)

    total = pl.pallas_call(
        functools.partial(near_kernel, n_col),
        out_shape=shape((rows, width), jnp.float32),
        in_specs=[VMEM] * (n_col + 1),
        out_specs=VMEM,
        compiler_params=PARAMS,
        name="near",
    )(*blocks, near)
    packed, *sends = pl.pallas_call(
        functools.partial(far_kernel, n_col, dense),
        out_shape=[shape((width, width), jnp.float32)]
        + [shape((wide, rows), jnp.bfloat16)] * n_col,
        in_specs=[VMEM] * (n_col + 3),
        out_specs=[VMEM] * (n_col + 1),
        scratch_shapes=[
            pltpu.VMEM((width, rows), jnp.bfloat16),
            pltpu.VMEM((width, width), jnp.float32),
        ],
        compiler_params=PARAMS,
        name="far",
    )(*blocks, far, total, own)

    col = lax.axis_index("col")
    panel = jnp.zeros((n_col, wide, rows), jnp.bfloat16)
    for distance in range(n_col):
        piece = sends[distance]
        if distance:
            piece = swap(piece, "col", distance)
        panel = lax.dynamic_update_index_in_dim(panel, piece, col ^ distance, 0)

    axes = ("row", "col")
    if dense:
        packed = packed.reshape(n_row * n_col, 4, LANES)
        packed = lax.all_to_all(packed, axes, 0, 0, tiled=True)
        diag_block = pl.pallas_call(
            close_kernel,
            out_shape=shape((n_col * tall, wide), jnp.float32),
            in_specs=[VMEM, VMEM],
            out_specs=VMEM,
            compiler_params=PARAMS,
            name="close",
        )(packed.reshape(width, width), diag_inv.reshape(n_col * tall, wide))
        return panel, diag_block.reshape(n_col, tall, wide)
    packed = packed.reshape(n_row, tall, n_col, wide).transpose(0, 2, 1, 3)
    packed = packed.reshape(n_row * n_col, 1, tall * wide)
    packed = lax.all_to_all(packed, axes, 0, 0, tiled=True)
    return panel, diag_inv + packed.reshape(n_row, n_col, tall, wide).sum(0)


def solution(mesh):
    return jax.shard_map(
        on_device,
        mesh=mesh,
        in_specs=(P("row", "col"), P("col", "row", None), P("col", "row"), P(None, "row", "col")),
        out_specs=(P(None, "col", "row"), P(None, "row", "col")),
        check_vma=False,
    )
```

```python
import functools

import jax
import jax.numpy as jnp
from jax import lax
from jax.experimental import pallas as pl
from jax.experimental.pallas import tpu as pltpu
from jax.sharding import PartitionSpec as P


VMEM = pl.BlockSpec(memory_space=pltpu.VMEM)
PARAMS = pltpu.CompilerParams(vmem_limit_bytes=16 * 2**20)
LANES = 128
ROUTES = {1: (0, 1), 2: (0, 2), 3: (2, 1), 4: (0, 4), 5: (4, 1), 6: (4, 2), 7: (0, 7)}


def in_hbm(array):
    return pltpu.with_memory_space_constraint(array, pltpu.HBM)


def swap(block, axis, distance):
    size = lax.axis_size(axis)
    return lax.ppermute(block, axis, [(i, i ^ distance) for i in range(size)])


def routes(distance, n_row):
    if n_row == 8:
        return ROUTES[distance]
    return (distance - 1, 1) if distance % 2 else (0, distance)


def mask_kernel(pattern_ref, factor_ref, inv_ref, own_ref, kept_ref, keep_ref, rows_ref, sem):
    width = factor_ref.shape[2]
    kept = pltpu.make_async_copy(inv_ref, kept_ref, sem.at[2])
    copies = (
        pltpu.make_async_copy(factor_ref, rows_ref, sem.at[0]),
        pltpu.make_async_copy(pattern_ref, keep_ref, sem.at[1]),
    )
    for copy in copies:
        copy.start()
    kept.start()
    for copy in copies:
        copy.wait()
    for block in range(keep_ref.shape[1]):
        rows = pl.ds(block * width, width)
        keep = keep_ref[0, block].astype(jnp.float32).astype(jnp.bfloat16)
        own_ref[rows, :] = rows_ref[0, rows, :] * keep
    kept.wait()


def add_products(total, blocks, level_ref, half):
    col = lax.axis_index("col")
    rows = level_ref.shape[1]
    pairs = blocks[0].shape[1] // (2 * rows)
    for distance, block_ref in enumerate(blocks):
        for pair in range(pairs):
            start = pl.multiple_of((2 * pair + half) * rows, rows)
            part = jnp.dot(
                block_ref[:, pl.ds(start, rows)],
                level_ref[(col ^ distance) * pairs + pair],
                preferred_element_type=jnp.float32,
            )
            total = part if total is None else total + part
    return total


def fill(level_ref, held_refs, first):
    row = lax.axis_index("row")
    for i, held_ref in enumerate(held_refs):
        level_ref[(row ^ (2 * i + first)) // 2] = held_ref[...]


def near_kernel(n_col, *refs):
    blocks, held, (total_ref, level_ref) = refs[:n_col], refs[n_col:-2], refs[-2:]
    fill(level_ref, held, 0)
    half = lax.axis_index("row") % 2
    total_ref[...] = add_products(None, blocks, level_ref, half)


def far_kernel(n_col, dense, *refs):
    blocks = refs[:n_col]
    near_ref, own_ref = refs[n_col : n_col + 2]
    held, refs = refs[n_col + 2 : -4 - n_col], refs[-4 - n_col :]
    packed_ref, sends = refs[0], refs[1 : 1 + n_col]
    turned_ref, inner_ref, level_ref = refs[1 + n_col :]
    fill(level_ref, held, 1)
    col = lax.axis_index("col")
    total = add_products(near_ref[...], blocks, level_ref, 1 - lax.axis_index("row") % 2)

    tall = turned_ref.shape[0] // n_col
    turned_ref[...] = jnp.transpose(-total).astype(jnp.bfloat16)
    for distance in range(n_col):
        start = pl.multiple_of((col ^ distance) * tall, tall)
        sends[distance][...] = turned_ref[pl.ds(start, tall), :]

    high = total.astype(jnp.bfloat16)
    low = (total - high.astype(jnp.float32)).astype(jnp.bfloat16)
    own = own_ref[...]
    dims = (((0,), (0,)), ((), ()))
    inner = lax.dot_general(own, high, dims, preferred_element_type=jnp.float32)
    inner += lax.dot_general(own, low, dims, preferred_element_type=jnp.float32)
    if not dense:
        packed_ref[...] = inner
        return
    inner_ref[...] = inner
    lane = lax.broadcasted_iota(jnp.int32, (8, LANES), 1) // 32
    for a in range(4):
        parts = [inner_ref[pl.ds(4 * a + b, 8, stride=16), :] for b in range(4)]
        for owner in range(4):
            piece = parts[owner]
            for b in range(4):
                if b != owner:
                    turned = pltpu.roll(parts[b], (b - owner) % 4 * 32, 1)
                    piece = jnp.where(lane == b, turned, piece)
            packed_ref[pl.ds(4 * owner + a, 8, stride=16), :] = piece


def close_kernel(packed_ref, diag_ref, out_ref):
    total = packed_ref[pl.ds(0, 16), :]
    for row in range(1, 8):
        total += packed_ref[pl.ds(16 * row, 16), :]
    for b in range(4):
        part = pltpu.roll(total, (4 - b) % 4 * 32, 1) if b else total
        rows = pl.ds(b, 16, stride=4)
        out_ref[rows, :] = diag_ref[rows, :] + part[:, :32]


def on_device(inv_blocks, factor, pattern, diag_inv):
    n_row = lax.axis_size("row")
    n_col = lax.axis_size("col")
    rows, width = factor.shape[1:]
    tall, wide = width // n_row, width // n_col
    dense = (width, n_row, n_col) == (LANES, 8, 4)
    shape = jax.ShapeDtypeStruct

    own, kept = pl.pallas_call(
        mask_kernel,
        out_shape=[
            shape((rows, width), jnp.bfloat16),
            shape(inv_blocks.shape, jnp.bfloat16),
        ],
        in_specs=[pl.BlockSpec(memory_space=pltpu.HBM)] * 3,
        out_specs=[VMEM] * 2,
        scratch_shapes=[
            pltpu.SMEM(pattern.shape, pattern.dtype),
            pltpu.VMEM(factor.shape, factor.dtype),
            pltpu.SemaphoreType.DMA((3,)),
        ],
        compiler_params=PARAMS,
        name="mask",
    )(in_hbm(pattern), in_hbm(factor), in_hbm(inv_blocks))

    blocks = [None] * n_col
    blocks[0] = kept
    for distance in range(2, n_col, 2):
        blocks[distance] = swap(kept, "col", distance)
    for distance in range(0, n_col, 2):
        blocks[distance + 1] = swap(blocks[distance], "col", 1)

    held = {0: own}
    for distance in sorted(range(1, n_row), key=lambda d: (routes(d, n_row)[0] != 0, d)):
        relay, hop = routes(distance, n_row)
        held[distance] = swap(held[relay], "row", hop)

    level = pltpu.VMEM((n_row // 2, rows, width), jnp.bfloat16)
    total = pl.pallas_call(
        functools.partial(near_kernel, n_col),
        out_shape=shape((rows, width), jnp.float32),
        in_specs=[VMEM] * (n_col + n_row // 2),
        out_specs=VMEM,
        scratch_shapes=[level],
        compiler_params=PARAMS,
        name="near",
    )(*blocks, *(held[d] for d in range(0, n_row, 2)))
    packed, *sends = pl.pallas_call(
        functools.partial(far_kernel, n_col, dense),
        out_shape=[shape((width, width), jnp.float32)]
        + [shape((wide, rows), jnp.bfloat16)] * n_col,
        in_specs=[VMEM] * (n_col + 2 + n_row // 2),
        out_specs=[VMEM] * (n_col + 1),
        scratch_shapes=[
            pltpu.VMEM((width, rows), jnp.bfloat16),
            pltpu.VMEM((width, width), jnp.float32),
            level,
        ],
        compiler_params=PARAMS,
        name="far",
    )(*blocks, total, own, *(held[d] for d in range(1, n_row, 2)))

    col = lax.axis_index("col")
    panel = jnp.zeros((n_col, wide, rows), jnp.bfloat16)
    for distance in range(n_col):
        piece = sends[distance]
        if distance:
            piece = swap(piece, "col", distance)
        panel = lax.dynamic_update_index_in_dim(panel, piece, col ^ distance, 0)

    axes = ("row", "col")
    if dense:
        packed = packed.reshape(n_row * n_col, 4, LANES)
        packed = lax.all_to_all(packed, axes, 0, 0, tiled=True)
        diag_block = pl.pallas_call(
            close_kernel,
            out_shape=shape((n_col * tall, wide), jnp.float32),
            in_specs=[VMEM, VMEM],
            out_specs=VMEM,
            compiler_params=PARAMS,
            name="close",
        )(packed.reshape(width, width), diag_inv.reshape(n_col * tall, wide))
        return panel, diag_block.reshape(n_col, tall, wide)
    packed = packed.reshape(n_row, tall, n_col, wide).transpose(0, 2, 1, 3)
    packed = packed.reshape(n_row * n_col, 1, tall * wide)
    packed = lax.all_to_all(packed, axes, 0, 0, tiled=True)
    return panel, diag_inv + packed.reshape(n_row, n_col, tall, wide).sum(0)


def solution(mesh):
    step = jax.shard_map(
        on_device,
        mesh=mesh,
        in_specs=(P("row", "col"), P("col", "row", None), P("col", "row"), P(None, "row", "col")),
        out_specs=(P(None, "col", "row"), P(None, "row", "col")),
        check_vma=False,
    )
    if dict(mesh.shape) != {"row": 8, "col": 4}:
        return step
    return step
```

```python
import functools

import jax
import jax.numpy as jnp
from jax import lax
from jax.experimental import pallas as pl
from jax.experimental.pallas import tpu as pltpu
from jax.sharding import PartitionSpec as P


VMEM = pl.BlockSpec(memory_space=pltpu.VMEM)
PARAMS = pltpu.CompilerParams(vmem_limit_bytes=16 * 2**20)
LANES = 128
ROUTES = {1: (0, 1), 2: (0, 2), 3: (2, 1), 4: (0, 4), 5: (4, 1), 6: (4, 2), 7: (0, 7)}


def in_hbm(array):
    return pltpu.with_memory_space_constraint(array, pltpu.HBM)


def swap(block, axis, distance):
    size = lax.axis_size(axis)
    return lax.ppermute(block, axis, [(i, i ^ distance) for i in range(size)])


def routes(distance, n_row):
    if n_row == 8:
        return ROUTES[distance]
    return (distance - 1, 1) if distance % 2 else (0, distance)


def mask_kernel(pattern_ref, factor_ref, inv_ref, own_ref, kept_ref, keep_ref, rows_ref, sem):
    width = factor_ref.shape[2]
    kept = pltpu.make_async_copy(inv_ref, kept_ref, sem.at[2])
    copies = (
        pltpu.make_async_copy(factor_ref, rows_ref, sem.at[0]),
        pltpu.make_async_copy(pattern_ref, keep_ref, sem.at[1]),
    )
    for copy in copies:
        copy.start()
    kept.start()
    for copy in copies:
        copy.wait()
    for block in range(keep_ref.shape[1]):
        rows = pl.ds(block * width, width)
        keep = keep_ref[0, block].astype(jnp.float32).astype(jnp.bfloat16)
        own_ref[rows, :] = rows_ref[0, rows, :] * keep
    kept.wait()


def add_products(total, blocks, level_ref, half):
    col = lax.axis_index("col")
    rows = level_ref.shape[1]
    pairs = blocks[0].shape[1] // (2 * rows)
    for distance, block_ref in enumerate(blocks):
        for pair in range(pairs):
            start = pl.multiple_of((2 * pair + half) * rows, rows)
            part = jnp.dot(
                block_ref[:, pl.ds(start, rows)],
                level_ref[(col ^ distance) * pairs + pair],
                preferred_element_type=jnp.float32,
            )
            total = part if total is None else total + part
    return total


def fill(level_ref, held_refs, first):
    row = lax.axis_index("row")
    for i, held_ref in enumerate(held_refs):
        level_ref[(row ^ (2 * i + first)) // 2] = held_ref[...]


def near_kernel(n_col, *refs):
    blocks, held, (total_ref, level_ref) = refs[:n_col], refs[n_col:-2], refs[-2:]
    fill(level_ref, held, 0)
    half = lax.axis_index("row") % 2
    total_ref[...] = add_products(None, blocks, level_ref, half)


def far_kernel(n_col, dense, *refs):
    blocks = refs[:n_col]
    near_ref, own_ref = refs[n_col : n_col + 2]
    held, (packed_ref, total_ref, inner_ref, level_ref) = refs[n_col + 2 : -4], refs[-4:]
    fill(level_ref, held, 1)
    total = add_products(near_ref[...], blocks, level_ref, 1 - lax.axis_index("row") % 2)
    total_ref[...] = total

    high = total.astype(jnp.bfloat16)
    low = (total - high.astype(jnp.float32)).astype(jnp.bfloat16)
    own = own_ref[...]
    dims = (((0,), (0,)), ((), ()))
    inner = lax.dot_general(own, high, dims, preferred_element_type=jnp.float32)
    inner += lax.dot_general(own, low, dims, preferred_element_type=jnp.float32)
    if not dense:
        packed_ref[...] = inner
        return
    inner_ref[...] = inner
    lane = lax.broadcasted_iota(jnp.int32, (8, LANES), 1) // 32
    for a in range(4):
        parts = [inner_ref[pl.ds(4 * a + b, 8, stride=16), :] for b in range(4)]
        for owner in range(4):
            piece = parts[owner]
            for b in range(4):
                if b != owner:
                    turned = pltpu.roll(parts[b], (b - owner) % 4 * 32, 1)
                    piece = jnp.where(lane == b, turned, piece)
            packed_ref[pl.ds(4 * owner + a, 8, stride=16), :] = piece


def turn_kernel(total_ref, *refs):
    sends, turned_ref = refs[:-1], refs[-1]
    col = lax.axis_index("col")
    tall = sends[0].shape[0]
    turned_ref[...] = jnp.transpose(-total_ref[...]).astype(jnp.bfloat16)
    for distance, send_ref in enumerate(sends):
        start = pl.multiple_of((col ^ distance) * tall, tall)
        send_ref[...] = turned_ref[pl.ds(start, tall), :]


def close_kernel(packed_ref, diag_ref, out_ref):
    total = packed_ref[pl.ds(0, 16), :]
    for row in range(1, 8):
        total += packed_ref[pl.ds(16 * row, 16), :]
    for b in range(4):
        part = pltpu.roll(total, (4 - b) % 4 * 32, 1) if b else total
        rows = pl.ds(b, 16, stride=4)
        out_ref[rows, :] = diag_ref[rows, :] + part[:, :32]


def on_device(inv_blocks, factor, pattern, diag_inv):
    n_row = lax.axis_size("row")
    n_col = lax.axis_size("col")
    rows, width = factor.shape[1:]
    tall, wide = width // n_row, width // n_col
    dense = (width, n_row, n_col) == (LANES, 8, 4)
    shape = jax.ShapeDtypeStruct

    own, kept = pl.pallas_call(
        mask_kernel,
        out_shape=[
            shape((rows, width), jnp.bfloat16),
            shape(inv_blocks.shape, jnp.bfloat16),
        ],
        in_specs=[pl.BlockSpec(memory_space=pltpu.HBM)] * 3,
        out_specs=[VMEM] * 2,
        scratch_shapes=[
            pltpu.SMEM(pattern.shape, pattern.dtype),
            pltpu.VMEM(factor.shape, factor.dtype),
            pltpu.SemaphoreType.DMA((3,)),
        ],
        compiler_params=PARAMS,
        name="mask",
    )(in_hbm(pattern), in_hbm(factor), in_hbm(inv_blocks))

    blocks = [None] * n_col
    blocks[0] = kept
    for distance in range(2, n_col, 2):
        blocks[distance] = swap(kept, "col", distance)
    for distance in range(0, n_col, 2):
        blocks[distance + 1] = swap(blocks[distance], "col", 1)

    held = {0: own}
    for distance in sorted(range(1, n_row), key=lambda d: (routes(d, n_row)[0] != 0, d)):
        relay, hop = routes(distance, n_row)
        held[distance] = swap(held[relay], "row", hop)

    level = pltpu.VMEM((n_row // 2, rows, width), jnp.bfloat16)
    total = pl.pallas_call(
        functools.partial(near_kernel, n_col),
        out_shape=shape((rows, width), jnp.float32),
        in_specs=[VMEM] * (n_col + n_row // 2),
        out_specs=VMEM,
        scratch_shapes=[level],
        compiler_params=PARAMS,
        name="near",
    )(*blocks, *(held[d] for d in range(0, n_row, 2)))
    packed, total = pl.pallas_call(
        functools.partial(far_kernel, n_col, dense),
        out_shape=[
            shape((width, width), jnp.float32),
            shape((rows, width), jnp.float32),
        ],
        in_specs=[VMEM] * (n_col + 2 + n_row // 2),
        out_specs=[VMEM] * 2,
        scratch_shapes=[pltpu.VMEM((width, width), jnp.float32), level],
        compiler_params=PARAMS,
        name="far",
    )(*blocks, total, own, *(held[d] for d in range(1, n_row, 2)))
    sends = pl.pallas_call(
        turn_kernel,
        out_shape=[shape((wide, rows), jnp.bfloat16)] * n_col,
        in_specs=[VMEM],
        out_specs=[VMEM] * n_col,
        scratch_shapes=[pltpu.VMEM((width, rows), jnp.bfloat16)],
        compiler_params=PARAMS,
        name="turn",
    )(total)

    col = lax.axis_index("col")
    panel = jnp.zeros((n_col, wide, rows), jnp.bfloat16)
    for distance in range(n_col):
        piece = sends[distance]
        if distance:
            piece = swap(piece, "col", distance)
        panel = lax.dynamic_update_index_in_dim(panel, piece, col ^ distance, 0)

    axes = ("row", "col")
    if dense:
        packed = packed.reshape(n_row * n_col, 4, LANES)
        packed = lax.all_to_all(packed, axes, 0, 0, tiled=True)
        diag_block = pl.pallas_call(
            close_kernel,
            out_shape=shape((n_col * tall, wide), jnp.float32),
            in_specs=[VMEM, VMEM],
            out_specs=VMEM,
            compiler_params=PARAMS,
            name="close",
        )(packed.reshape(width, width), diag_inv.reshape(n_col * tall, wide))
        return panel, diag_block.reshape(n_col, tall, wide)
    packed = packed.reshape(n_row, tall, n_col, wide).transpose(0, 2, 1, 3)
    packed = packed.reshape(n_row * n_col, 1, tall * wide)
    packed = lax.all_to_all(packed, axes, 0, 0, tiled=True)
    return panel, diag_inv + packed.reshape(n_row, n_col, tall, wide).sum(0)


def solution(mesh):
    step = jax.shard_map(
        on_device,
        mesh=mesh,
        in_specs=(P("row", "col"), P("col", "row", None), P("col", "row"), P(None, "row", "col")),
        out_specs=(P(None, "col", "row"), P(None, "row", "col")),
        check_vma=False,
    )
    if dict(mesh.shape) != {"row": 8, "col": 4}:
        return step
    return step
```
